32 devices in a mesh: seq: 16 (over z, y, x), tp: 2 (over core).
Axes of the slice: x: 2, y: 2, z: 4, core: 2. Of those that a mesh axis runs over, the one named last changes fastest.
Arguments:
- node_features: bfloat16 [8192, 1024], P('seq'), may hold values from -16 to 16
- cluster_ids: int32 [8192], P('seq'), may hold values from 0 to 31
- neighbors: int32 [16, 3], replicated, may hold values from 0 to 15, as said below
- qkv_weight: bfloat16 [1024, 3, 1024], P(None, None, 'tp'), may hold values from -0.1875 to 0.1875
- out_weight: bfloat16 [1024, 1024], P('tp'), may hold values from -0.1875 to 0.1875
- virtual_gain: float32 [1024], replicated, may hold values from 0.1 to 1.9
Outputs:
- layer_output: bfloat16 [8192, 1024], P(('seq', 'tp'))
- virtual_tokens: bfloat16 [32, 1024], P('seq')
The draws below stay inside these ranges and needn't reach their ends.
Inputs may be any that keep to these rules, and one draw needn't show every extreme that they name: `neighbors`: each row names three distinct blocks, none of them the row's own block, all in the same aligned run of 8 blocks as the row's block.
All inputs are finite; a program needn't handle non-finite values.
Results may differ from the reference program's by a relative error of at most 0.012.
The reference program's roundings to bfloat16 on the way (of `projected`, `virtual_pairs`, `queries`, `weights` and `attended`) count: a program that leaves them out, or rounds other values in their place, can miss the bound.
Values may be sent and summed in bfloat16 or wider, within the bound.
A program may use at most 128 MiB of HBM per device.

```python
import math
import jax
import jax.numpy as jnp
from jax import lax

D = 1024
HEADS = 16
BLOCK = 512
BLOCKS_DEV = 1
VIRT_DEV = 2
HEAD_GROUP = 8
NODES = 8192
NBLOCKS = 16
VIRTUAL = 32


def draw_node_features(key, part):
    first_key, second_key, third_key = jax.random.split(jax.random.fold_in(key, 11), 3)
    base_values = jax.random.truncated_normal(first_key, -4.0, 4.0, (NODES, D), jnp.float32)
    row_scale = jnp.exp(jax.random.uniform(second_key, (NODES, 1), jnp.float32, math.log(0.5), math.log(2.0)))
    column_scale = jnp.exp(jax.random.uniform(third_key, (1, D), jnp.float32, math.log(0.5), math.log(2.0)))
    return (base_values * row_scale * column_scale).astype(jnp.bfloat16)


def draw_cluster_ids(key, part):
    first_key, second_key, third_key = jax.random.split(jax.random.fold_in(key, 23), 3)
    owner_dev = jnp.arange(NODES, dtype=jnp.int32) // (BLOCKS_DEV * BLOCK)
    local_pick = jax.random.randint(first_key, (NODES,), 0, VIRT_DEV, dtype=jnp.int32)
    any_pick = jax.random.randint(second_key, (NODES,), 0, VIRTUAL, dtype=jnp.int32)
    stays_home = jax.random.randint(third_key, (NODES,), 0, 4, dtype=jnp.int32) < 3
    return jnp.where(stays_home, owner_dev * VIRT_DEV + local_pick, any_pick).astype(jnp.int32)


def draw_neighbors(key, part):
    run_blocks = HEAD_GROUP * BLOCKS_DEV
    random_part = jax.random.randint(jax.random.fold_in(key, 37), (NBLOCKS, run_blocks - 1), 0, 1 << 20, dtype=jnp.int32)
    priority = random_part * run_blocks + jnp.arange(run_blocks - 1, dtype=jnp.int32)[None, :]
    top_values, picked = lax.top_k(priority, 3)
    offsets = picked.astype(jnp.int32) + 1
    block_ids = jnp.arange(NBLOCKS, dtype=jnp.int32)[:, None]
    run_start = block_ids // run_blocks * run_blocks
    return (run_start + (block_ids - run_start + offsets) % run_blocks).astype(jnp.int32)


def shard_levels(stream_key, shape, pieces, smallest, high):
    factor_of, own = 1.0, jax.random.fold_in(stream_key, 6)
    for axis_at, parts in pieces:
        steps = jnp.exp(jax.random.uniform(jax.random.fold_in(own, axis_at), (parts,), jnp.float32, smallest / len(pieces), high / len(pieces)))
        factor_of = factor_of * jnp.repeat(steps, shape[axis_at] // parts).reshape([-1 if axis == axis_at else 1 for axis in range(len(shape))])
    return factor_of


def normal_values(own_key, extent, spread, bound, cuts=(), kind=jnp.bfloat16):
    entries = jax.random.normal(own_key, extent, jnp.float32) * spread
    if len(cuts) > 0:
        entries = shard_levels(own_key, extent, cuts, -0.22, 0.18) * entries
    return jnp.clip(entries, min=-bound, max=bound).astype(kind)


def setup_inputs(seed: int = 0) -> dict:
    key_list = jax.random.split(jax.random.key(seed), 7)
    node_features = draw_node_features(jax.random.fold_in(key_list[6], 71), 0)
    cluster_ids = draw_cluster_ids(jax.random.fold_in(key_list[6], 71), 0)
    neighbors = draw_neighbors(jax.random.fold_in(key_list[6], 71), 0)
    qkv_weight = normal_values(key_list[3], (D, 3, D), D ** -0.5, 0.1875, ((2, 2),))
    out_weight = normal_values(key_list[4], (D, D), D ** -0.5, 0.1875, ((0, 2),))
    virtual_gain = jnp.clip(1.0 + 0.18 * jax.random.normal(key_list[5], (D,), jnp.float32), 0.1, 1.9)
    return dict(node_features=node_features, cluster_ids=cluster_ids, neighbors=neighbors, qkv_weight=qkv_weight, out_weight=out_weight, virtual_gain=virtual_gain)


epsilon = 1e-06
sharpness = 2.5

def row_norm(values):
    return values * lax.rsqrt(lax.optimization_barrier(jnp.mean(values * values, axis=-1, keepdims=True)) + epsilon)

def reference(node_features, cluster_ids, neighbors, qkv_weight, out_weight, virtual_gain):
    head_size = D // HEADS
    query_scale = sharpness / math.sqrt(head_size)
    projected = jnp.dot(node_features, qkv_weight.reshape(D, 3 * D), preferred_element_type=jnp.float32).astype(jnp.bfloat16)
    projected = projected.reshape(NODES, 3, HEADS, head_size)
    pooled = jax.ops.segment_sum(node_features.astype(jnp.float32), cluster_ids, num_segments=VIRTUAL)
    virtual_tokens = (row_norm(pooled) * virtual_gain).astype(jnp.bfloat16)
    virtual_pairs = jnp.dot(virtual_tokens, qkv_weight[:, 1:, :].reshape(D, 2 * D), preferred_element_type=jnp.float32).astype(jnp.bfloat16)
    virtual_pairs = virtual_pairs.reshape(VIRTUAL, 2, HEADS, head_size)
    queries = (row_norm(projected[:, 0].astype(jnp.float32)) * query_scale).astype(jnp.bfloat16).reshape(NBLOCKS, BLOCK, HEADS, head_size)
    normed_keys = row_norm(projected[:, 1].astype(jnp.float32)).astype(jnp.bfloat16).reshape(NBLOCKS, BLOCK, HEADS, head_size)
    values = projected[:, 2].reshape(NBLOCKS, BLOCK, HEADS, head_size)
    virtual_keys = row_norm(virtual_pairs[:, 0].astype(jnp.float32)).astype(jnp.bfloat16)
    virtual_values = virtual_pairs[:, 1]

    def one_block(block_id):
        chosen = jnp.concatenate([block_id[None], neighbors[block_id]]).astype(jnp.int32)
        key_rows = jnp.concatenate([normed_keys[chosen].reshape(4 * BLOCK, HEADS, head_size), virtual_keys], axis=0).astype(jnp.float32)
        value_rows = jnp.concatenate([values[chosen].reshape(4 * BLOCK, HEADS, head_size), virtual_values], axis=0).astype(jnp.float32)
        scores = jnp.einsum('qhd,khd->hqk', queries[block_id].astype(jnp.float32), key_rows, precision=lax.Precision.HIGHEST)
        raised = jnp.exp(scores)
        weights = (raised / lax.optimization_barrier(jnp.sum(raised, axis=-1, keepdims=True))).astype(jnp.bfloat16)
        mixed_heads = jnp.einsum('hqk,khd->qhd', weights.astype(jnp.float32), value_rows, precision=lax.Precision.HIGHEST).astype(jnp.bfloat16)
        return mixed_heads.reshape(BLOCK, D)
    attended = lax.map(one_block, jnp.arange(NBLOCKS, dtype=jnp.int32)).reshape(NODES, D)
    layer_output = jnp.dot(attended, out_weight, preferred_element_type=jnp.float32).astype(jnp.bfloat16)
    return (layer_output, virtual_tokens)
```

```python
import functools
import math

import jax
import jax.numpy as jnp
from jax import lax
from jax.experimental import pallas as pl
from jax.experimental.pallas import tpu as pltpu
from jax.sharding import PartitionSpec as P

VIRT_DEV = 2
LANES = 128

epsilon = 1e-06
sharpness = 2.5

MESH = pl.DeviceIdType.MESH
F32 = jnp.float32
BF16 = jnp.bfloat16


def flip(index, offset, size):
    out = index * 0
    bit = 1
    while bit < size:
        own = index // bit % 2
        out = out + bit * ((1 - own) if offset & bit else own)
        bit *= 2
    return out


def flip_traced(index, offset, size):
    out = index * 0
    bit = 1
    while bit < size:
        own = index // bit % 2
        other = offset // bit % 2
        out = out + bit * ((own + other) % 2)
        bit *= 2
    return out


def kernel(
    n_seq, group, head,
    x_hbm, ids_ref, nb_ref, w_hbm, ow_hbm, gain_ref,
    out_ref, tok_ref,
    x_ref, w_q, w_kv, ow_ref,
    kv_send, kv_recv, q_send, q_recv, vx, vkx, vvx,
    pool_send, pool_recv, tok_send, tok_recv, vall, ow_other, ret_send, ret_recv,
    in_sem, unit_sem,
    a_ssem, a_rsem, q_ssem, q_rsem, p_ssem, p_rsem, t_ssem, t_rsem, o_ssem, o_rsem, r_ssem, r_rsem,
):
    seq = lax.axis_index("seq")
    core = lax.axis_index("tp")
    g = seq % group
    base = seq - g
    rows, width = x_ref.shape
    half = rows // 2
    quarter = rows // 4
    virt = VIRT_DEV * n_seq
    scale = sharpness / math.sqrt(head)
    units = group // 2

    barrier = pltpu.get_barrier_semaphore()

    def loop(count, body):
        def run(step, carry):
            body(step)
            return carry

        lax.fori_loop(0, count, run, 0)

    loop(
        n_seq - 1,
        lambda step: pl.semaphore_signal(
            barrier, inc=1, device_id=((seq + 1 + step) % n_seq, core), device_id_type=MESH
        ),
    )
    loop(
        group,
        lambda step: pl.semaphore_signal(
            barrier, inc=1, device_id=(base + step, 1 - core), device_id_type=MESH
        ),
    )

    x_load = pltpu.make_async_copy(x_hbm, x_ref, in_sem.at[0])
    x_load.start()
    unit_loads = []
    for u in range(units):
        pair = flip(g // 2, u, units)
        cols = pl.ds(pl.multiple_of(pair * LANES, LANES), LANES)
        unit_loads.append(
            pltpu.make_async_copy(w_hbm.at[pl.ds(1, 2), :, cols], w_kv.at[u], unit_sem.at[u])
        )
        unit_loads[u].start()
    q_load = pltpu.make_async_copy(w_hbm.at[0], w_q, in_sem.at[1])
    q_load.start()
    ow_load = pltpu.make_async_copy(ow_hbm, ow_ref, in_sem.at[2])
    ow_load.start()

    lane = lax.broadcasted_iota(jnp.int32, (rows, LANES), 1)
    low = lane < head
    low_half = low[:half]
    seg_a = lax.broadcasted_iota(jnp.int32, (LANES, LANES), 0) // head
    seg_b = lax.broadcasted_iota(jnp.int32, (LANES, LANES), 1) // head
    ones_block = (seg_a == seg_b).astype(F32).astype(BF16)

    def normed(values):
        square = values * values
        hi = square.astype(BF16)
        lo = (square - hi.astype(F32)).astype(BF16)
        total = jnp.dot(hi, ones_block, preferred_element_type=F32) + jnp.dot(
            lo, ones_block, preferred_element_type=F32
        )
        return values * lax.rsqrt(total * (1.0 / head) + epsilon)

    def a_copy(o):
        peer = flip(g, o, group)
        return pltpu.make_async_remote_copy(
            src_ref=kv_send.at[peer], dst_ref=kv_recv.at[g],
            send_sem=a_ssem.at[o], recv_sem=a_rsem.at[o],
            device_id=(base + peer, core), device_id_type=MESH,
        )

    def q_copy(o, peer):
        return pltpu.make_async_remote_copy(
            src_ref=q_send.at[peer], dst_ref=q_recv.at[g],
            send_sem=q_ssem.at[o], recv_sem=q_rsem.at[o],
            device_id=(base + peer, core), device_id_type=MESH,
        )

    def p_copy(step):
        peer = (seq + 1 + step) % n_seq
        return pltpu.make_async_remote_copy(
            src_ref=pool_send.at[peer], dst_ref=pool_recv.at[step],
            send_sem=p_ssem.at[step], recv_sem=p_rsem.at[step],
            device_id=(peer, core), device_id_type=MESH,
        )

    def t_copy(step):
        peer = (seq + 1 + step) % n_seq
        return pltpu.make_async_remote_copy(
            src_ref=tok_send, dst_ref=tok_recv.at[seq],
            send_sem=t_ssem.at[step], recv_sem=t_rsem.at[step],
            device_id=(peer, core), device_id_type=MESH,
        )

    o_copy = pltpu.make_async_remote_copy(
        src_ref=ow_ref, dst_ref=ow_other, send_sem=o_ssem, recv_sem=o_rsem,
        device_id=(seq, 1 - core), device_id_type=MESH,
    )

    x_load.wait()
    member = (
        lax.broadcasted_iota(jnp.int32, (virt, rows), 0) == jnp.broadcast_to(ids_ref[...], (virt, rows))
    ).astype(F32).astype(BF16)
    pool = jnp.dot(member, x_ref[...], preferred_element_type=F32)
    for p in range(n_seq):
        pool_send[p] = pool[VIRT_DEV * p : VIRT_DEV * (p + 1), :]

    def project(u):
        pair = flip(g // 2, u, units)
        unit_loads[u].wait()
        weights = jnp.concatenate([w_kv[u, 0], w_kv[u, 1]], axis=1)
        kv = jnp.dot(x_ref[...], weights, preferred_element_type=F32).astype(BF16).astype(F32)
        k, v = normed(kv[:, :LANES]), kv[:, LANES:]
        kv_send[pair * 2] = jnp.where(low, k, pltpu.roll(v, head, 1)).astype(BF16)
        kv_send[pair * 2 + 1] = jnp.where(low, pltpu.roll(k, head, 1), v).astype(BF16)

    early = [1 << bit for bit in range(group.bit_length() - 1)]
    if group > 2:
        early.append(group - 1)
    late = [o for o in range(group - 1, 0, -1) if o not in early]
    done = set()
    for o in early:
        if o // 2 not in done:
            project(o // 2)
        if not done:
            pl.semaphore_wait(barrier, n_seq - 1 + group)
            loop(n_seq - 1, lambda step: p_copy(step).start())
        done.add(o // 2)
        a_copy(o).start()
    for u in range(units):
        if u not in done:
            project(u)

    for o in late:
        a_copy(o).start()
    q_load.wait()
    for i in range(units):
        q = jnp.dot(
            x_ref[...], w_q[:, i * LANES : (i + 1) * LANES], preferred_element_type=F32
        ).astype(BF16).astype(F32)
        q = normed(q) * scale
        top, bottom = q[:half], q[half:]
        q_send[2 * i] = jnp.where(low_half, top, pltpu.roll(bottom, head, 1)).astype(BF16)
        q_send[2 * i + 1] = jnp.where(low_half, pltpu.roll(top, head, 1), bottom).astype(BF16)

    loop(n_seq - 1, lambda step: p_copy(step).wait())
    pool_recv[n_seq - 1] = pool_send[seq]

    def add(step, total):
        return total + pool_recv[(seq + n_seq - 1 - step) % n_seq]

    pooled = lax.fori_loop(0, n_seq, add, jnp.zeros((VIRT_DEV, width), F32))
    tokens = pooled * lax.rsqrt(jnp.mean(pooled * pooled, axis=-1, keepdims=True) + epsilon)
    tokens = (tokens * gain_ref[...]).astype(BF16)
    tok_ref[...] = tokens
    tok_send[...] = tokens.astype(F32)
    tok_recv[seq] = tokens.astype(F32)
    loop(n_seq - 1, lambda step: t_copy(step).start())
    for o in range(group - 1, 0, -1):
        q_copy(o, flip(g, o, group)).start()
    ow_load.wait()
    o_copy.start()

    def spread(block):
        vx[block] = jnp.where(low, 1.0, kv_recv[block].astype(F32)).astype(BF16)

    kv_recv[g] = kv_send[g]
    q_recv[g] = q_send[g]
    spread(g)
    for o in early + late:
        a_copy(o).wait()
        spread(flip(g, o, group))

    def r_copy(o, block, e):
        to_core = (core + e) % 2
        return pltpu.make_async_remote_copy(
            src_ref=ret_send.at[block, to_core], dst_ref=ret_recv.at[core, g],
            send_sem=r_ssem.at[e, o], recv_sem=r_rsem.at[e, o],
            device_id=(base + block, to_core), device_id_type=MESH,
        )

    def piece(query, key_rows, value_rows):
        scores = lax.dot_general(
            query, key_rows, (((1,), (1,)), ((), ())), preferred_element_type=F32
        )
        raised = jnp.exp(scores).astype(BF16)
        return jnp.dot(raised, value_rows, preferred_element_type=F32)

    def receive_virtual():
        loop(n_seq - 1, lambda step: t_copy(step).wait())
        for p in range(n_seq):
            vall[VIRT_DEV * p : VIRT_DEV * (p + 1), :] = tok_recv[p]
        weights = jnp.concatenate([w_kv[0, 0], w_kv[0, 1]], axis=1)
        pairs = jnp.dot(vall[...].astype(BF16), weights, preferred_element_type=F32)
        pairs = pairs.astype(BF16).astype(F32)
        vk, vv = normed(pairs[:, :LANES]), pairs[:, LANES:]
        odd = jnp.broadcast_to(g % 2, (virt, LANES)) == 1
        vlow = lax.broadcasted_iota(jnp.int32, (virt, LANES), 1) < head
        vk = jnp.where(odd, pltpu.roll(vk, head, 1), vk)
        vkx[...] = jnp.where(vlow, vk, 0.0).astype(BF16)
        vv = jnp.where(odd, vv, pltpu.roll(vv, head, 1))
        vvx[...] = jnp.where(vlow, 1.0, vv).astype(BF16)

    def one_block(o):
        o = (group - o) % group
        block = flip_traced(g, o, group)

        @pl.when(o != 0)
        def _():
            q_copy(o, block).wait()

        packed = q_recv[block].astype(F32)
        query = jnp.concatenate(
            [
                jnp.where(low_half, packed, 0.0),
                jnp.where(low_half, pltpu.roll(packed, head, 1), 0.0),
            ],
            axis=0,
        ).astype(BF16)
        total = piece(query, kv_recv[block], vx[block])
        for j in range(nb_ref.shape[0]):
            other = nb_ref[j, base + block] % group
            total = total + piece(query, kv_recv[other], vx[other])

        total = total + piece(query, vkx[...], vvx[...])
        mixed = total / pltpu.roll(total, head, 1)
        shifted = pltpu.roll(mixed, head, 1)
        for t in range(2):
            first = shifted[t * half : t * half + quarter]
            second = mixed[t * half + quarter : (t + 1) * half]
            ret_send[block, t] = jnp.where(low[:quarter], first, second).astype(BF16)

        r_copy(o, block, 1).start()

        @pl.when(o != 0)
        def _():
            r_copy(o, block, 0).start()

    receive_virtual()
    loop(group, one_block)
    ret_recv[core, g] = ret_send[g, core]

    o_copy.wait()
    for o in range(group):
        for e in range(2):
            if o or e:
                r_copy(o, flip(g, o, group), e).wait()

    lowq = low[:quarter]

    def gathered(side):
        tops, bottoms = [], []
        for i in range(units):
            a = ret_recv[side, 2 * i].astype(F32)
            b = ret_recv[side, 2 * i + 1].astype(F32)
            tops.append(jnp.where(lowq, a, pltpu.roll(b, head, 1)).astype(BF16))
            bottoms.append(jnp.where(lowq, pltpu.roll(a, head, 1), b).astype(BF16))
        return jnp.concatenate(
            [jnp.concatenate(tops, axis=1), jnp.concatenate(bottoms, axis=1)], axis=0
        )

    result = jnp.dot(gathered(core), ow_ref[...], preferred_element_type=F32)
    result = result + jnp.dot(gathered(1 - core), ow_other[...], preferred_element_type=F32)
    out_ref[...] = result.astype(BF16)


def solution(mesh):
    n_seq = mesh.shape["seq"]

    def body(node_features, cluster_ids, neighbors, qkv_weight, out_weight, virtual_gain):
        rows, width = node_features.shape
        local = qkv_weight.shape[2]
        head = LANES // 2
        group = local // head
        virt = VIRT_DEV * n_seq
        vmem = pl.BlockSpec(memory_space=pltpu.VMEM)
        any_ = pl.BlockSpec(memory_space=pl.ANY)
        dma = pltpu.SemaphoreType.DMA
        return pl.pallas_call(
            functools.partial(kernel, n_seq, group, head),
            out_shape=(
                jax.ShapeDtypeStruct((rows // 2, width), BF16),
                jax.ShapeDtypeStruct((VIRT_DEV, width), BF16),
            ),
            in_specs=[any_, vmem, pl.BlockSpec(memory_space=pltpu.SMEM), any_, any_, vmem],
            out_specs=(vmem, vmem),
            scratch_shapes=[
                pltpu.VMEM((rows, width), BF16),
                pltpu.VMEM((width, local), BF16),
                pltpu.VMEM((group // 2, 2, width, LANES), BF16),
                pltpu.VMEM((local, width), BF16),
                pltpu.VMEM((group, rows, LANES), BF16),
                pltpu.VMEM((group, rows, LANES), BF16),
                pltpu.VMEM((group, rows // 2, LANES), BF16),
                pltpu.VMEM((group, rows // 2, LANES), BF16),
                pltpu.VMEM((group, rows, LANES), BF16),
                pltpu.VMEM((virt, LANES), BF16),
                pltpu.VMEM((virt, LANES), BF16),
                pltpu.VMEM((n_seq, VIRT_DEV, width), F32),
                pltpu.VMEM((n_seq, VIRT_DEV, width), F32),
                pltpu.VMEM((VIRT_DEV, width), F32),
                pltpu.VMEM((n_seq, VIRT_DEV, width), F32),
                pltpu.VMEM((virt, width), F32),
                pltpu.VMEM((local, width), BF16),
                pltpu.VMEM((group, 2, rows // 4, LANES), BF16),
                pltpu.VMEM((2, group, rows // 4, LANES), BF16),
                dma((3,)),
                dma((group // 2,)),
                dma((group,)),
                dma((group,)),
                dma((group,)),
                dma((group,)),
                dma((n_seq,)),
                dma((n_seq,)),
                dma((n_seq,)),
                dma((n_seq,)),
                dma,
                dma,
                dma((2, group)),
                dma((2, group)),
            ],
            compiler_params=pltpu.CompilerParams(
                collective_id=0, has_side_effects=True, vmem_limit_bytes=60 * 1024 * 1024
            ),
        )(
            node_features,
            cluster_ids.reshape(1, rows),
            neighbors.T,
            qkv_weight.transpose(1, 0, 2),
            out_weight,
            virtual_gain.reshape(1, width),
        )

    return jax.shard_map(
        body,
        mesh=mesh,
        in_specs=(P("seq", None), P("seq"), P(), P(None, None, "tp"), P("tp", None), P()),
        out_specs=(P(("seq", "tp"), None), P("seq", None)),
        check_vma=False,
    )
```
